32 devices in a mesh: lon: 8 (over y, x, core), spec: 4 (over z).
Axes of the slice: x: 2, y: 2, z: 4, core: 2. Of those that a mesh axis runs over, the one named last changes fastest.
Arguments:
- lam_final: float32 [1296, 64, 1024], P('spec', None, 'lon'), may hold values from -6 to 6
- stored_source: bfloat16 [2, 1296, 64, 1024], P(None, 'spec', None, 'lon'), may hold values from 0.19921875 to 1.1953125
- mixing: bfloat16 [1296, 1296], replicated, may hold values from -0.15625 to 0.15625
- drift_x: float32 [1296], replicated, may hold values from -0.45 to 0.45
- drift_y: float32 [1296], replicated, may hold values from -0.45 to 0.45
- ocean_mask: int32 [64, 1024], P(None, 'lon'), may hold values 0 or 1
- misfit: float32 [2, 64, 1024], P(None, None, 'lon'), may hold values from -6 to 6
- obs_mask: int32 [2, 64, 1024], P(None, None, 'lon'), may hold values 0 or 1
Outputs:
- lam_start: float32 [1296, 64, 1024], P('spec', None, 'lon')
The draws below stay inside these ranges and needn't reach their ends.
All inputs are finite; a program needn't handle non-finite values. No bound on the sum of `ocean_mask` or of `obs_mask` on one device may be relied on, other than what follows from the above.
Results may differ from the reference program's by a relative error of at most 0.0028.
Values may be sent and summed in bfloat16 or wider, within the bound.
A program may use at most 192 MiB of HBM per device.

```python
import jax
import jax.numpy as jnp
from jax import lax

LAT = 64
STEPS = 2
K = 1296
LONW = 1024


def with_ends(array, key, smallest, largest):
    place = [jax.random.randint(jax.random.fold_in(key, axis), (), 0, length) for axis, length in enumerate(array.shape)]
    longest = array.shape.index(max(array.shape))
    neighbour = place[:longest] + [(place[longest] + 1) % array.shape[longest]] + place[longest + 1:]
    return array.at[tuple(place)].set(smallest).at[tuple(neighbour)].set(largest)


def steps_of(stream_key, dims, pieces, low, largest):
    def one(position, parts):
        steps = jax.random.uniform(jax.random.fold_in(jax.random.fold_in(stream_key, 6), position), (parts,), jnp.float32, low / len(pieces), largest / len(pieces))
        return jnp.repeat(jnp.exp(steps), dims[position] // parts).reshape((-1,) + (1,) * (len(dims) - position - 1))

    loudness = one(*pieces[0])
    for cut in pieces[1:]:
        loudness = loudness * one(*cut)
    return loudness


def bell_draw(own_key, extent, scale, most, cuts=(), dtype=jnp.bfloat16):
    loudness = steps_of(own_key, extent, cuts, -0.22, 0.18) if cuts else 1.0
    array = jax.random.normal(own_key, extent, jnp.float32) * scale * loudness
    return jnp.minimum(jnp.maximum(array, -most), most).astype(dtype)


def setup_inputs(seed: int = 0) -> dict:
    splits = jax.random.split(jax.random.key(seed), 9)
    lam_final = bell_draw(splits[0], (K, LAT, LONW), 1.0, 6.0, ((0, 4), (2, 8)), jnp.float32)
    stored_source = jnp.clip(0.19921875 + 0.99609375 * jax.random.uniform(splits[1], (STEPS, K, LAT, LONW), jnp.float32) ** steps_of(splits[1], (STEPS, K, LAT, LONW), ((1, 4), (3, 8)), -0.2, 0.2), 0.19921875, 1.1953125).astype(jnp.bfloat16)
    mixing = bell_draw(splits[2], (K, K), K ** -0.5, 0.15625)
    drift_x = jnp.clip(jax.random.uniform(splits[3], (K,), jnp.float32, -0.45, 0.45), -0.45, 0.45)
    drift_y = jnp.clip(jax.random.uniform(splits[4], (K,), jnp.float32, -0.45, 0.45), -0.45, 0.45)
    ocean_mask = with_ends((jax.random.randint(splits[5], (LAT, LONW), 0, 4) < 3).astype(jnp.int32), jax.random.fold_in(splits[5], 1), 0, 1)
    misfit = bell_draw(splits[6], (STEPS, LAT, LONW), 1.0, 6.0, ((2, 8),), jnp.float32)
    obs_mask = with_ends((jax.random.randint(splits[7], (STEPS, LAT, LONW), 0, 3) < 1).astype(jnp.int32), jax.random.fold_in(splits[7], 1), 0, 1)
    return {"lam_final": lam_final, "stored_source": stored_source, "mixing": mixing, "drift_x": drift_x, "drift_y": drift_y, "ocean_mask": ocean_mask, "misfit": misfit, "obs_mask": obs_mask}


def couple_terms(adjoint, mixing):
    rounded = adjoint.astype(jnp.bfloat16)
    flat = rounded.reshape(rounded.shape[0], -1).astype(jnp.float32)
    coupled = lax.dot_general(mixing.astype(jnp.float32), flat, (((0,), (0,)), ((), ())), precision=lax.Precision.HIGHEST, preferred_element_type=jnp.float32)
    coupled = lax.optimization_barrier(coupled.astype(jnp.bfloat16))
    return coupled.astype(jnp.float32).reshape(adjoint.shape)


def advect_back(adjoint, drift_x, drift_y):
    speed_x = drift_x[:, None, None]
    speed_y = drift_y[:, None, None]
    eastern = jnp.roll(adjoint, -1, axis=2)
    western = jnp.roll(adjoint, 1, axis=2)
    zero_row = jnp.zeros_like(adjoint[:, :1])
    northern = jnp.concatenate([adjoint[:, 1:], zero_row], axis=1)
    southern = jnp.concatenate([zero_row, adjoint[:, :-1]], axis=1)
    stay = 1.0 - jnp.abs(speed_x) - jnp.abs(speed_y)
    result = stay * adjoint + jnp.maximum(speed_x, 0.0) * eastern + jnp.maximum(-speed_x, 0.0) * western
    return result + jnp.maximum(speed_y, 0.0) * northern + jnp.maximum(-speed_y, 0.0) * southern


def reference(lam_final, stored_source, mixing, drift_x, drift_y, ocean_mask, misfit, obs_mask):
    ocean_field = ocean_mask.astype(jnp.float32)[None]
    adjoint = lam_final
    for step_index in reversed(range(STEPS)):
        forcing = misfit[step_index] * obs_mask[step_index].astype(jnp.float32)
        adjoint = (adjoint + forcing[None]) * ocean_field
        adjoint = adjoint + stored_source[step_index].astype(jnp.float32) * couple_terms(adjoint, mixing)
        adjoint = advect_back(adjoint, drift_x, drift_y)
    return adjoint
```

```python
import functools

import jax
import jax.numpy as jnp
from jax import lax
from jax.experimental import pallas as pl
from jax.experimental.pallas import tpu as pltpu
from jax.sharding import PartitionSpec as P

CHUNKS = 4
MESH = pl.DeviceIdType.MESH


def chunk_bounds(own):
    inner = [int(round(own * q / CHUNKS / 16)) * 16 for q in range(1, CHUNKS)]
    edges = [0] + inner + [own]
    return list(zip(edges[:-1], edges[1:]))


def round_up(value, unit):
    return -(-value // unit) * unit


def group_of(count):
    return 4 if count % 4 == 0 else (2 if count % 2 == 0 else 1)


def kernel(
    steps, parts, ring, bounds, own_pad,
    lam, source, weights, drift_x, drift_y, ocean_mask, misfit, obs_mask,
    out,
    state, send_in, recv_in, send_out, recv_out, flat, weight_buf, spread, unpack,
    source_buf, halo_send, halo_recv,
    send_sem, recv_sem, halo_send_sem, halo_recv_sem, lam_sem, source_sem, weight_sem, out_sem,
):
    me = lax.axis_index("spec")
    lon = lax.axis_index("lon")
    own, lat, width = state.shape
    rows = lat // parts
    east, west = lax.rem(lon + 1, ring), lax.rem(lon + ring - 1, ring)
    chunks = len(bounds)
    peers = list(range(1, parts))
    order = [(step, q) for step in reversed(range(steps)) for q in range(chunks)]

    def peer(offset):
        return lax.rem(me + offset, parts)

    def lam_copy(q):
        low, high = bounds[q]
        return pltpu.make_async_copy(
            lam.at[pl.ds(low, high - low)], state.at[pl.ds(low, high - low)], lam_sem.at[q]
        )

    def source_copy(position):
        step, q = order[position]
        low, high = bounds[q]
        slot = position % 2
        return pltpu.make_async_copy(
            source.at[step, pl.ds(low, high - low)],
            source_buf.at[slot, pl.ds(0, high - low)],
            source_sem.at[slot],
        )

    def out_copy(q):
        low, high = bounds[q]
        return pltpu.make_async_copy(
            state.at[pl.ds(low, high - low)], out.at[pl.ds(low, high - low)], out_sem.at[q]
        )

    weight_copy = pltpu.make_async_copy(weights, weight_buf, weight_sem)

    def exchange(phase, q, offset):
        low, high = bounds[q]
        sender, receiver = (send_in, recv_in) if phase == 0 else (send_out, recv_out)
        target = peer(offset)
        return pltpu.make_async_remote_copy(
            src_ref=sender.at[target, pl.ds(low, high - low)],
            dst_ref=receiver.at[me, pl.ds(low, high - low)],
            send_sem=send_sem.at[phase, q, offset - 1],
            recv_sem=recv_sem.at[phase, q, me],
            device_id={"spec": target},
            device_id_type=MESH,
        )

    def arrival(phase, q, offset):
        low, high = bounds[q]
        sender, receiver = (send_in, recv_in) if phase == 0 else (send_out, recv_out)
        origin = peer(offset)
        return pltpu.make_async_remote_copy(
            src_ref=sender.at[origin, pl.ds(low, high - low)],
            dst_ref=receiver.at[origin, pl.ds(low, high - low)],
            send_sem=send_sem.at[phase, q, offset - 1],
            recv_sem=recv_sem.at[phase, q, origin],
            device_id={"spec": origin},
            device_id_type=MESH,
        )

    def halo(position, side):
        return pltpu.make_async_remote_copy(
            src_ref=halo_send.at[position, side],
            dst_ref=halo_recv.at[position, side],
            send_sem=halo_send_sem.at[position, side],
            recv_sem=halo_recv_sem.at[position, side],
            device_id={"lon": west if side == 0 else east},
            device_id_type=MESH,
        )

    for q in range(chunks):
        lam_copy(q).start()
    weight_copy.start()
    source_copy(0).start()
    source_copy(1).start()

    barrier = pltpu.get_barrier_semaphore()
    for offset in peers:
        pl.semaphore_signal(barrier, inc=1, device_id={"spec": peer(offset)}, device_id_type=MESH)
    for side in (west, east):
        pl.semaphore_signal(barrier, inc=1, device_id={"lon": side}, device_id_type=MESH)
    pl.semaphore_wait(barrier, len(peers) + 2)

    ocean = ocean_mask[...].astype(jnp.float32)
    row = lax.broadcasted_iota(jnp.int32, (lat, width), 0)
    lane = lax.broadcasted_iota(jnp.int32, (lat, width), 1)

    def forcing_of(step):
        return misfit[step] * obs_mask[step].astype(jnp.float32)

    def emit(adjoint, c):
        state[c] = adjoint
        rounded = adjoint.astype(jnp.bfloat16)
        for part in range(parts):
            send_in[part, c] = rounded[part * rows : (part + 1) * rows]

    forcing = forcing_of(steps - 1)
    for q in range(chunks):
        low, high = bounds[q]
        lam_copy(q).wait()

        def prepare(c, carry):
            emit((state[c] + forcing) * ocean, c)
            return carry

        lax.fori_loop(low, high, prepare, 0)
        for offset in peers:
            exchange(0, q, offset).start()

    for step in reversed(range(steps)):
        last = step == 0

        for q in range(chunks):
            low, high = bounds[q]
            count = high - low
            padded = round_up(count, 16)
            group = group_of(count)

            for offset in range(parts):
                origin = peer(offset)
                if offset:
                    arrival(0, q, offset).wait_recv()
                block = recv_in if offset else send_in
                if padded != count:
                    unpack[pl.ds(count * rows, (padded - count) * rows)] = jnp.zeros(
                        ((padded - count) * rows, width), jnp.float32
                    )

                def widen(t, carry):
                    value = block[origin, pl.ds(low + t * group, group)]
                    unpack[pl.ds(pl.multiple_of(t * group * rows, 8), group * rows)] = value.astype(
                        jnp.float32
                    ).reshape(group * rows, width)
                    return carry

                lax.fori_loop(0, count // group, widen, 0)
                base = pl.multiple_of(origin * own_pad + low, 16)
                for i in range(rows):
                    flat[pl.ds(base, padded), pl.ds(i * width, width)] = unpack[
                        pl.ds(i, padded, stride=rows)
                    ].astype(jnp.bfloat16)

        if step == steps - 1:
            weight_copy.wait()
        start = 0
        for q in range(chunks):
            low, high = bounds[q]
            count = high - low
            tall = round_up(count, 8)
            group = group_of(count)
            total = parts * tall

            def multiply(pair, carry):
                columns = pl.ds(pl.multiple_of(pair * 2 * width, 2 * width), 2 * width)
                result = jnp.dot(
                    weight_buf[start : start + total],
                    flat[:, columns],
                    preferred_element_type=jnp.float32,
                )
                spread[pl.ds(pair * 2, total, stride=rows)] = result[:, :width]
                spread[pl.ds(pair * 2 + 1, total, stride=rows)] = result[:, width:]
                return carry

            lax.fori_loop(0, rows // 2, multiply, 0)
            if not step == steps - 1:
                for offset in peers:
                    exchange(1, q, offset).wait_send()
            for part in range(parts):

                def narrow(t, carry):
                    place = pl.multiple_of((part * tall + t * group) * rows, 8)
                    value = spread[pl.ds(place, group * rows)]
                    send_out[part, pl.ds(low + t * group, group)] = value.reshape(
                        group, rows, width
                    ).astype(jnp.bfloat16)
                    return carry

                lax.fori_loop(0, count // group, narrow, 0)
            for offset in peers:
                exchange(1, q, offset).start()
            recv_out[me, pl.ds(low, count)] = send_out[me, pl.ds(low, count)]
            start += total

        forcing = None if last else forcing_of(step - 1)
        for q in range(chunks):
            low, high = bounds[q]
            count = high - low
            position = (steps - 1 - step) * chunks + q
            slot = position % 2
            source_copy(position).wait()
            for offset in peers:
                arrival(1, q, offset).wait_recv()

            def update(c, carry):
                to_west, to_east = carry
                coupled = jnp.concatenate(
                    [recv_out[part, c].astype(jnp.float32) for part in range(parts)], axis=0
                )
                factor = source_buf[slot, c - low].astype(jnp.float32)
                adjoint = state[c] + factor * coupled
                state[c] = adjoint
                to_west = jnp.where(lane == 0, adjoint, pltpu.roll(to_west, 1, 1))
                to_east = jnp.where(lane == width - 1, adjoint, pltpu.roll(to_east, width - 1, 1))
                return to_west, to_east

            zero = jnp.zeros((lat, width), jnp.float32)
            to_west, to_east = lax.fori_loop(low, high, update, (zero, zero))
            halo_send[position, 0] = to_west
            halo_send[position, 1] = to_east
            halo(position, 0).start()
            halo(position, 1).start()
            if position + 2 < len(order):
                source_copy(position + 2).start()
            if not last:
                for offset in peers:
                    exchange(0, q, offset).wait_send()
            halo(position, 0).wait()
            halo(position, 1).wait()

            def advect(c, carry):
                from_east, from_west = carry
                adjoint = state[c]
                speed_x = drift_x[me * own + c]
                speed_y = drift_y[me * own + c]
                eastern = jnp.where(lane == width - 1, from_east, pltpu.roll(adjoint, width - 1, 1))
                western = jnp.where(lane == 0, from_west, pltpu.roll(adjoint, 1, 1))
                northern = jnp.where(row == lat - 1, 0.0, pltpu.roll(adjoint, lat - 1, 0))
                southern = jnp.where(row == 0, 0.0, pltpu.roll(adjoint, 1, 0))
                stay = 1.0 - jnp.abs(speed_x) - jnp.abs(speed_y)
                result = (
                    stay * adjoint
                    + jnp.maximum(speed_x, 0.0) * eastern
                    + jnp.maximum(-speed_x, 0.0) * western
                )
                result = (
                    result
                    + jnp.maximum(speed_y, 0.0) * northern
                    + jnp.maximum(-speed_y, 0.0) * southern
                )
                if last:
                    state[c] = result
                else:
                    emit((result + forcing) * ocean, c)
                return pltpu.roll(from_east, 1, 1), pltpu.roll(from_west, width - 1, 1)

            from_east = pltpu.roll(halo_recv[position, 0], (width - count) % width, 1)
            from_west = pltpu.roll(halo_recv[position, 1], count % width, 1)
            lax.fori_loop(low, high, advect, (from_east, from_west))
            if last:
                out_copy(q).start()
            else:
                for offset in peers:
                    exchange(0, q, offset).start()

    for q in range(chunks):
        for offset in peers:
            exchange(0, q, offset).wait_send()
            exchange(1, q, offset).wait_send()
        out_copy(q).wait()


def arrange_weights(mixing, parts, own, own_pad, bounds):
    table = mixing.T.reshape(parts, own, parts, own)
    table = jnp.pad(table, ((0, 0), (0, 0), (0, 0), (0, own_pad - own)))
    pieces = []
    for low, high in bounds:
        tall = round_up(high - low, 8)
        piece = jnp.pad(table[:, low:high], ((0, 0), (0, tall - (high - low)), (0, 0), (0, 0)))
        pieces.append(piece.reshape(parts * tall, parts * own_pad))
    return jnp.concatenate(pieces, axis=0)


def per_device(
    parts, ring, lam_final, stored_source, mixing, drift_x, drift_y, ocean_mask, misfit, obs_mask
):
    steps = stored_source.shape[0]
    own, lat, width = lam_final.shape
    rows = lat // parts
    bounds = chunk_bounds(own)
    own_pad = round_up(own, 16)
    largest = max(high - low for low, high in bounds)
    weights = arrange_weights(mixing, parts, own, own_pad, bounds)
    vmem = pl.BlockSpec(memory_space=pltpu.VMEM)
    smem = pl.BlockSpec(memory_space=pltpu.SMEM)
    hbm = pl.BlockSpec(memory_space=pl.ANY)
    block = pltpu.VMEM((parts, own, rows, width), jnp.bfloat16)
    dma = pltpu.SemaphoreType.DMA
    positions = steps * CHUNKS
    return pl.pallas_call(
        functools.partial(kernel, steps, parts, ring, bounds, own_pad),
        out_shape=jax.ShapeDtypeStruct(lam_final.shape, jnp.float32),
        in_specs=[hbm, hbm, hbm, smem, smem, vmem, vmem, vmem],
        out_specs=hbm,
        scratch_shapes=[
            pltpu.VMEM((own, lat, width), jnp.float32),
            block, block, block, block,
            pltpu.VMEM((parts * own_pad, rows * width), jnp.bfloat16),
            pltpu.VMEM(weights.shape, jnp.bfloat16),
            pltpu.VMEM((parts * round_up(largest, 8) * rows, width), jnp.float32),
            pltpu.VMEM((round_up(largest, 16) * rows, width), jnp.float32),
            pltpu.VMEM((2, largest, lat, width), jnp.bfloat16),
            pltpu.VMEM((positions, 2, lat, width), jnp.float32),
            pltpu.VMEM((positions, 2, lat, width), jnp.float32),
            dma((2, CHUNKS, parts - 1)),
            dma((2, CHUNKS, parts)),
            dma((positions, 2)),
            dma((positions, 2)),
            dma((CHUNKS,)),
            dma((2,)),
            dma,
            dma((CHUNKS,)),
        ],
        compiler_params=pltpu.CompilerParams(
            collective_id=0, has_side_effects=True, vmem_limit_bytes=60 * 1024 * 1024
        ),
    )(lam_final, stored_source, weights, drift_x, drift_y, ocean_mask, misfit, obs_mask)


def solution(mesh):
    in_specs = (
        P("spec", None, "lon"),
        P(None, "spec", None, "lon"),
        P(),
        P(),
        P(),
        P(None, "lon"),
        P(None, None, "lon"),
        P(None, None, "lon"),
    )
    out_specs = P("spec", None, "lon")
    return jax.shard_map(
        functools.partial(per_device, mesh.shape["spec"], mesh.shape["lon"]),
        mesh=mesh, in_specs=in_specs, out_specs=out_specs, check_vma=False,
    )
```

```python
import functools

import jax
import jax.numpy as jnp
from jax import lax
from jax.experimental import pallas as pl
from jax.experimental.pallas import tpu as pltpu
from jax.sharding import PartitionSpec as P

CHUNKS = 4
MESH = pl.DeviceIdType.MESH


def chunk_bounds(own):
    inner = [int(round(own * q / CHUNKS / 16)) * 16 for q in range(1, CHUNKS)]
    edges = [0] + inner + [own]
    return list(zip(edges[:-1], edges[1:]))


def round_up(value, unit):
    return -(-value // unit) * unit


def group_of(count):
    return 4 if count % 4 == 0 else (2 if count % 2 == 0 else 1)


def kernel(
    steps, parts, ring, bounds, own_pad,
    lam, source, mixing, drift_x, drift_y, ocean_mask, misfit, obs_mask,
    out,
    state, send_in, recv_in, send_out, recv_out, flat, mixing_buf, arranged, weight_buf, spread, unpack,
    source_buf, halo_send, halo_recv,
    send_sem, recv_sem, halo_send_sem, halo_recv_sem, lam_sem, source_sem, weight_sem, out_sem,
):
    me = lax.axis_index("spec")
    lon = lax.axis_index("lon")
    own, lat, width = state.shape
    rows = lat // parts
    east, west = lax.rem(lon + 1, ring), lax.rem(lon + ring - 1, ring)
    chunks = len(bounds)
    peers = list(range(parts - 1))
    half = max(parts // 2, 1)
    order = [(step, q) for step in reversed(range(steps)) for q in range(chunks)]

    def peer(index):
        if index < half:
            return half - lax.div(me, half) * half + lax.rem(me + index, half)
        return lax.div(me, half) * half + lax.rem(me + index - half + 1, half)

    def lam_copy(q):
        low, high = bounds[q]
        return pltpu.make_async_copy(
            lam.at[pl.ds(low, high - low)], state.at[pl.ds(low, high - low)], lam_sem.at[q]
        )

    def source_copy(position):
        step, q = order[position]
        low, high = bounds[q]
        slot = position % 2
        return pltpu.make_async_copy(
            source.at[step, pl.ds(low, high - low)],
            source_buf.at[slot, pl.ds(0, high - low)],
            source_sem.at[slot],
        )

    def out_copy(q):
        low, high = bounds[q]
        return pltpu.make_async_copy(
            state.at[pl.ds(low, high - low)], out.at[pl.ds(low, high - low)], out_sem.at[q]
        )

    mixing_copy = pltpu.make_async_copy(mixing, mixing_buf, weight_sem)

    def exchange(phase, q, offset):
        low, high = bounds[q]
        sender, receiver = (send_in, recv_in) if phase == 0 else (send_out, recv_out)
        target = peer(offset)
        return pltpu.make_async_remote_copy(
            src_ref=sender.at[target, pl.ds(low, high - low)],
            dst_ref=receiver.at[me, pl.ds(low, high - low)],
            send_sem=send_sem.at[phase, q, offset],
            recv_sem=recv_sem.at[phase, q, me],
            device_id={"spec": target},
            device_id_type=MESH,
        )

    def arrival(phase, q, offset):
        low, high = bounds[q]
        sender, receiver = (send_in, recv_in) if phase == 0 else (send_out, recv_out)
        origin = peer(offset)
        return pltpu.make_async_remote_copy(
            src_ref=sender.at[origin, pl.ds(low, high - low)],
            dst_ref=receiver.at[origin, pl.ds(low, high - low)],
            send_sem=send_sem.at[phase, q, offset],
            recv_sem=recv_sem.at[phase, q, origin],
            device_id={"spec": origin},
            device_id_type=MESH,
        )

    def halo(position, side):
        return pltpu.make_async_remote_copy(
            src_ref=halo_send.at[position, side],
            dst_ref=halo_recv.at[position, side],
            send_sem=halo_send_sem.at[position, side],
            recv_sem=halo_recv_sem.at[position, side],
            device_id={"lon": west if side == 0 else east},
            device_id_type=MESH,
        )

    for q in range(chunks):
        lam_copy(q).start()
    mixing_copy.start()
    source_copy(0).start()
    source_copy(1).start()

    barrier = pltpu.get_barrier_semaphore()
    for offset in peers:
        pl.semaphore_signal(barrier, inc=1, device_id={"spec": peer(offset)}, device_id_type=MESH)
    for side in (west, east):
        pl.semaphore_signal(barrier, inc=1, device_id={"lon": side}, device_id_type=MESH)
    pl.semaphore_wait(barrier, len(peers) + 2)

    ocean = ocean_mask[...].astype(jnp.float32)
    row = lax.broadcasted_iota(jnp.int32, (lat, width), 0)
    lane = lax.broadcasted_iota(jnp.int32, (lat, width), 1)

    def forcing_of(step):
        return misfit[step] * obs_mask[step].astype(jnp.float32)

    def emit(adjoint, c):
        state[c] = adjoint
        rounded = adjoint.astype(jnp.bfloat16)
        for part in range(parts):
            send_in[part, c] = rounded[part * rows : (part + 1) * rows]

    forcing = forcing_of(steps - 1)
    for q in range(chunks):
        low, high = bounds[q]
        lam_copy(q).wait()

        def prepare(c, carry):
            emit((state[c] + forcing) * ocean, c)
            return carry

        lax.fori_loop(low, high, prepare, 0)
        for offset in peers:
            exchange(0, q, offset).start()

    mixing_copy.wait()
    components = parts * own
    start = 0
    for q in range(chunks):
        low, high = bounds[q]
        tall = round_up(high - low, 16)
        piece_row = lax.broadcasted_iota(jnp.int32, (tall, components), 0)
        piece_column = lax.broadcasted_iota(jnp.int32, (tall, components), 1)

        def arrange(part, carry):
            wanted = (piece_column == part * own + low + piece_row) & (piece_row < high - low)
            arranged[pl.ds(pl.multiple_of(start + part * tall, 16), tall)] = lax.dot_general(
                wanted.astype(jnp.float32).astype(jnp.bfloat16),
                mixing_buf[...],
                (((1,), (1,)), ((), ())),
                preferred_element_type=jnp.float32,
            ).astype(jnp.bfloat16)
            return carry

        lax.fori_loop(0, parts, arrange, 0)
        start += parts * tall

    def spread_columns(origin, carry):
        pick_row = lax.broadcasted_iota(jnp.int32, (components, own_pad), 0)
        pick_column = lax.broadcasted_iota(jnp.int32, (components, own_pad), 1)
        pick = (pick_row == origin * own + pick_column) & (pick_column < own)
        mixing_buf[:, :own_pad] = pick.astype(jnp.float32).astype(jnp.bfloat16)
        block = weight_buf.shape[0] // 4

        def rows_of(t, inner):
            place = pl.ds(pl.multiple_of(t * block, 16), block)
            weight_buf[place, pl.ds(pl.multiple_of(origin * own_pad, 128), own_pad)] = jnp.dot(
                arranged[place], mixing_buf[:, :own_pad], preferred_element_type=jnp.float32
            ).astype(jnp.bfloat16)
            return inner

        return lax.fori_loop(0, 4, rows_of, carry)

    lax.fori_loop(0, parts, spread_columns, 0)

    for origin in range(parts):
        flat[origin * own_pad + own : (origin + 1) * own_pad] = jnp.zeros(
            (own_pad - own, rows * width), jnp.bfloat16
        )

    for step in reversed(range(steps)):
        last = step == 0

        for q in range(chunks):
            low, high = bounds[q]
            count = high - low
            padded = round_up(count, 16)
            group = group_of(count)

            for offset in [None] + peers:
                if offset is None:
                    origin, block = me, send_in
                else:
                    origin, block = peer(offset), recv_in
                    arrival(0, q, offset).wait_recv()
                if padded != count:
                    unpack[pl.ds(count * rows, (padded - count) * rows)] = jnp.zeros(
                        ((padded - count) * rows, width), jnp.float32
                    )

                def widen(t, carry):
                    value = block[origin, pl.ds(low + t * group, group)]
                    unpack[pl.ds(pl.multiple_of(t * group * rows, 8), group * rows)] = value.astype(
                        jnp.float32
                    ).reshape(group * rows, width)
                    return carry

                lax.fori_loop(0, count // group, widen, 0)
                base = pl.multiple_of(origin * own_pad + low, 16)
                for i in range(rows):
                    flat[pl.ds(base, padded), pl.ds(i * width, width)] = unpack[
                        pl.ds(i, padded, stride=rows)
                    ].astype(jnp.bfloat16)

        start = 0
        for q in range(chunks):
            low, high = bounds[q]
            count = high - low
            tall = round_up(count, 16)
            group = group_of(count)
            total = parts * tall

            def multiply(pair, carry):
                columns = pl.ds(pl.multiple_of(pair * 2 * width, 2 * width), 2 * width)
                result = jnp.dot(
                    weight_buf[start : start + total],
                    flat[:, columns],
                    preferred_element_type=jnp.float32,
                )
                spread[pl.ds(pair * 2, total, stride=rows)] = result[:, :width]
                spread[pl.ds(pair * 2 + 1, total, stride=rows)] = result[:, width:]
                return carry

            lax.fori_loop(0, rows // 2, multiply, 0)
            if not step == steps - 1:
                for offset in peers:
                    exchange(1, q, offset).wait_send()
            for part in range(parts):

                def narrow(t, carry):
                    place = pl.multiple_of((part * tall + t * group) * rows, 8)
                    value = spread[pl.ds(place, group * rows)]
                    send_out[part, pl.ds(low + t * group, group)] = value.reshape(
                        group, rows, width
                    ).astype(jnp.bfloat16)
                    return carry

                lax.fori_loop(0, count // group, narrow, 0)
            for offset in peers:
                exchange(1, q, offset).start()
            recv_out[me, pl.ds(low, count)] = send_out[me, pl.ds(low, count)]
            start += total

        forcing = None if last else forcing_of(step - 1)
        for q in range(chunks):
            low, high = bounds[q]
            count = high - low
            position = (steps - 1 - step) * chunks + q
            slot = position % 2
            source_copy(position).wait()
            for offset in peers:
                arrival(1, q, offset).wait_recv()

            def update(c, carry):
                to_west, to_east = carry
                coupled = jnp.concatenate(
                    [recv_out[part, c].astype(jnp.float32) for part in range(parts)], axis=0
                )
                factor = source_buf[slot, c - low].astype(jnp.float32)
                adjoint = state[c] + factor * coupled
                state[c] = adjoint
                to_west = jnp.where(lane == 0, adjoint, pltpu.roll(to_west, 1, 1))
                to_east = jnp.where(lane == width - 1, adjoint, pltpu.roll(to_east, width - 1, 1))
                return to_west, to_east

            zero = jnp.zeros((lat, width), jnp.float32)
            to_west, to_east = lax.fori_loop(low, high, update, (zero, zero))
            halo_send[position, 0] = to_west
            halo_send[position, 1] = to_east
            halo(position, 0).start()
            halo(position, 1).start()
            if position + 2 < len(order):
                source_copy(position + 2).start()
            if not last:
                for offset in peers:
                    exchange(0, q, offset).wait_send()
            halo(position, 0).wait()
            halo(position, 1).wait()

            def advect(c, carry):
                from_east, from_west = carry
                adjoint = state[c]
                speed_x = drift_x[me * own + c]
                speed_y = drift_y[me * own + c]
                eastern = jnp.where(lane == width - 1, from_east, pltpu.roll(adjoint, width - 1, 1))
                western = jnp.where(lane == 0, from_west, pltpu.roll(adjoint, 1, 1))
                northern = jnp.where(row == lat - 1, 0.0, pltpu.roll(adjoint, lat - 1, 0))
                southern = jnp.where(row == 0, 0.0, pltpu.roll(adjoint, 1, 0))
                stay = 1.0 - jnp.abs(speed_x) - jnp.abs(speed_y)
                result = (
                    stay * adjoint
                    + jnp.maximum(speed_x, 0.0) * eastern
                    + jnp.maximum(-speed_x, 0.0) * western
                )
                result = (
                    result
                    + jnp.maximum(speed_y, 0.0) * northern
                    + jnp.maximum(-speed_y, 0.0) * southern
                )
                if last:
                    state[c] = result
                else:
                    emit((result + forcing) * ocean, c)
                return pltpu.roll(from_east, 1, 1), pltpu.roll(from_west, width - 1, 1)

            from_east = pltpu.roll(halo_recv[position, 0], (width - count) % width, 1)
            from_west = pltpu.roll(halo_recv[position, 1], count % width, 1)
            lax.fori_loop(low, high, advect, (from_east, from_west))
            if last:
                out_copy(q).start()
            else:
                for offset in peers:
                    exchange(0, q, offset).start()

    for q in range(chunks):
        for offset in peers:
            exchange(0, q, offset).wait_send()
            exchange(1, q, offset).wait_send()
        out_copy(q).wait()


def per_device(
    parts, ring, lam_final, stored_source, mixing, drift_x, drift_y, ocean_mask, misfit, obs_mask
):
    steps = stored_source.shape[0]
    own, lat, width = lam_final.shape
    rows = lat // parts
    bounds = chunk_bounds(own)
    own_pad = round_up(own, 128)
    largest = max(high - low for low, high in bounds)
    tall = sum(round_up(high - low, 16) for low, high in bounds) * parts
    vmem = pl.BlockSpec(memory_space=pltpu.VMEM)
    smem = pl.BlockSpec(memory_space=pltpu.SMEM)
    hbm = pl.BlockSpec(memory_space=pl.ANY)
    block = pltpu.VMEM((parts, own, rows, width), jnp.bfloat16)
    dma = pltpu.SemaphoreType.DMA
    positions = steps * CHUNKS
    return pl.pallas_call(
        functools.partial(kernel, steps, parts, ring, bounds, own_pad),
        out_shape=jax.ShapeDtypeStruct(lam_final.shape, jnp.float32),
        in_specs=[hbm, hbm, hbm, smem, smem, vmem, vmem, vmem],
        out_specs=hbm,
        scratch_shapes=[
            pltpu.VMEM((own, lat, width), jnp.float32),
            block, block, block, block,
            pltpu.VMEM((parts * own_pad, rows * width), jnp.bfloat16),
            pltpu.VMEM(mixing.shape, jnp.bfloat16),
            pltpu.VMEM((tall, parts * own), jnp.bfloat16),
            pltpu.VMEM((tall, parts * own_pad), jnp.bfloat16),
            pltpu.VMEM((parts * round_up(largest, 16) * rows, width), jnp.float32),
            pltpu.VMEM((round_up(largest, 16) * rows, width), jnp.float32),
            pltpu.VMEM((2, largest, lat, width), jnp.bfloat16),
            pltpu.VMEM((positions, 2, lat, width), jnp.float32),
            pltpu.VMEM((positions, 2, lat, width), jnp.float32),
            dma((2, CHUNKS, parts - 1)),
            dma((2, CHUNKS, parts)),
            dma((positions, 2)),
            dma((positions, 2)),
            dma((CHUNKS,)),
            dma((2,)),
            dma,
            dma((CHUNKS,)),
        ],
        compiler_params=pltpu.CompilerParams(
            collective_id=0, has_side_effects=True, vmem_limit_bytes=60 * 1024 * 1024
        ),
    )(lam_final, stored_source, mixing, drift_x, drift_y, ocean_mask, misfit, obs_mask)


def solution(mesh):
    in_specs = (
        P("spec", None, "lon"),
        P(None, "spec", None, "lon"),
        P(),
        P(),
        P(),
        P(None, "lon"),
        P(None, None, "lon"),
        P(None, None, "lon"),
    )
    out_specs = P("spec", None, "lon")
    return jax.shard_map(
        functools.partial(per_device, mesh.shape["spec"], mesh.shape["lon"]),
        mesh=mesh, in_specs=in_specs, out_specs=out_specs, check_vma=False,
    )
```

```python
import functools

import jax
import jax.numpy as jnp
from jax import lax
from jax.experimental import pallas as pl
from jax.experimental.pallas import tpu as pltpu
from jax.sharding import PartitionSpec as P

SHARES = (0.15, 0.5, 0.85)
CHUNKS = len(SHARES) + 1
MESH = pl.DeviceIdType.MESH


def chunk_bounds(own):
    inner = [int(round(own * share / 16)) * 16 for share in SHARES]
    edges = [0] + inner + [own]
    return list(zip(edges[:-1], edges[1:]))


def round_up(value, unit):
    return -(-value // unit) * unit


def group_of(count):
    return 4 if count % 4 == 0 else (2 if count % 2 == 0 else 1)


def kernel(
    steps, parts, ring, bounds, own_pad,
    lam, source, mixing, drift_x, drift_y, ocean_mask, misfit, obs_mask,
    out,
    state, send_in, recv_in, send_out, recv_out, flat, mixing_buf, arranged, weight_buf, spread, unpack,
    source_buf, halo_send, halo_recv,
    send_sem, recv_sem, halo_send_sem, halo_recv_sem, lam_sem, source_sem, weight_sem, out_sem,
):
    me = lax.axis_index("spec")
    lon = lax.axis_index("lon")
    own, lat, width = state.shape
    rows = lat // parts
    east, west = lax.rem(lon + 1, ring), lax.rem(lon + ring - 1, ring)
    chunks = len(bounds)
    peers = list(range(parts - 1))
    half = max(parts // 2, 1)
    order = [(step, q) for step in reversed(range(steps)) for q in range(chunks)]

    def peer(index):
        if index < half:
            return half - lax.div(me, half) * half + lax.rem(me + index, half)
        return lax.div(me, half) * half + lax.rem(me + index - half + 1, half)

    def lam_copy(q):
        low, high = bounds[q]
        return pltpu.make_async_copy(
            lam.at[pl.ds(low, high - low)], state.at[pl.ds(low, high - low)], lam_sem.at[q]
        )

    def source_copy(position):
        step, q = order[position]
        low, high = bounds[q]
        slot = position % 2
        return pltpu.make_async_copy(
            source.at[step, pl.ds(low, high - low)],
            source_buf.at[slot, pl.ds(0, high - low)],
            source_sem.at[slot],
        )

    def out_copy(q):
        low, high = bounds[q]
        return pltpu.make_async_copy(
            state.at[pl.ds(low, high - low)], out.at[pl.ds(low, high - low)], out_sem.at[q]
        )

    mixing_copy = pltpu.make_async_copy(mixing, mixing_buf, weight_sem)

    def exchange(phase, q, offset):
        low, high = bounds[q]
        sender, receiver = (send_in, recv_in) if phase == 0 else (send_out, recv_out)
        target = peer(offset)
        return pltpu.make_async_remote_copy(
            src_ref=sender.at[target, pl.ds(low, high - low)],
            dst_ref=receiver.at[me, pl.ds(low, high - low)],
            send_sem=send_sem.at[phase, q, offset],
            recv_sem=recv_sem.at[phase, q, me],
            device_id={"spec": target},
            device_id_type=MESH,
        )

    def arrival(phase, q, offset):
        low, high = bounds[q]
        sender, receiver = (send_in, recv_in) if phase == 0 else (send_out, recv_out)
        origin = peer(offset)
        return pltpu.make_async_remote_copy(
            src_ref=sender.at[origin, pl.ds(low, high - low)],
            dst_ref=receiver.at[origin, pl.ds(low, high - low)],
            send_sem=send_sem.at[phase, q, offset],
            recv_sem=recv_sem.at[phase, q, origin],
            device_id={"spec": origin},
            device_id_type=MESH,
        )

    def halo(position, side):
        return pltpu.make_async_remote_copy(
            src_ref=halo_send.at[position, side],
            dst_ref=halo_recv.at[position, side],
            send_sem=halo_send_sem.at[position, side],
            recv_sem=halo_recv_sem.at[position, side],
            device_id={"lon": west if side == 0 else east},
            device_id_type=MESH,
        )

    for q in range(chunks):
        lam_copy(q).start()
    mixing_copy.start()
    source_copy(0).start()
    source_copy(1).start()

    barrier = pltpu.get_barrier_semaphore()
    for offset in peers:
        pl.semaphore_signal(barrier, inc=1, device_id={"spec": peer(offset)}, device_id_type=MESH)
    for side in (west, east):
        pl.semaphore_signal(barrier, inc=1, device_id={"lon": side}, device_id_type=MESH)
    pl.semaphore_wait(barrier, len(peers) + 2)

    ocean = ocean_mask[...].astype(jnp.float32)
    row = lax.broadcasted_iota(jnp.int32, (lat, width), 0)
    lane = lax.broadcasted_iota(jnp.int32, (lat, width), 1)

    def forcing_of(step):
        return misfit[step] * obs_mask[step].astype(jnp.float32)

    def emit(adjoint, c):
        state[c] = adjoint
        rounded = adjoint.astype(jnp.bfloat16)
        for part in range(parts):
            send_in[part, c] = rounded[part * rows : (part + 1) * rows]

    forcing = forcing_of(steps - 1)
    for q in range(chunks):
        low, high = bounds[q]
        lam_copy(q).wait()

        def prepare(c, carry):
            emit((state[c] + forcing) * ocean, c)
            return carry

        lax.fori_loop(low, high, prepare, 0)
        for offset in peers:
            exchange(0, q, offset).start()

    mixing_copy.wait()
    components = parts * own
    start = 0
    for q in range(chunks):
        low, high = bounds[q]
        tall = round_up(high - low, 16)
        piece_row = lax.broadcasted_iota(jnp.int32, (tall, components), 0)
        piece_column = lax.broadcasted_iota(jnp.int32, (tall, components), 1)

        def arrange(part, carry):
            wanted = (piece_column == part * own + low + piece_row) & (piece_row < high - low)
            arranged[pl.ds(pl.multiple_of(start + part * tall, 16), tall)] = lax.dot_general(
                wanted.astype(jnp.float32).astype(jnp.bfloat16),
                mixing_buf[...],
                (((1,), (1,)), ((), ())),
                preferred_element_type=jnp.float32,
            ).astype(jnp.bfloat16)
            return carry

        lax.fori_loop(0, parts, arrange, 0)
        start += parts * tall

    def spread_columns(origin, carry):
        pick_row = lax.broadcasted_iota(jnp.int32, (components, own_pad), 0)
        pick_column = lax.broadcasted_iota(jnp.int32, (components, own_pad), 1)
        pick = (pick_row == origin * own + pick_column) & (pick_column < own)
        mixing_buf[:, :own_pad] = pick.astype(jnp.float32).astype(jnp.bfloat16)
        block = weight_buf.shape[0] // 4

        def rows_of(t, inner):
            place = pl.ds(pl.multiple_of(t * block, 16), block)
            weight_buf[place, pl.ds(pl.multiple_of(origin * own_pad, 128), own_pad)] = jnp.dot(
                arranged[place], mixing_buf[:, :own_pad], preferred_element_type=jnp.float32
            ).astype(jnp.bfloat16)
            return inner

        return lax.fori_loop(0, 4, rows_of, carry)

    lax.fori_loop(0, parts, spread_columns, 0)

    for origin in range(parts):
        flat[origin * own_pad + own : (origin + 1) * own_pad] = jnp.zeros(
            (own_pad - own, rows * width), jnp.bfloat16
        )

    for step in reversed(range(steps)):
        last = step == 0

        for q in range(chunks):
            low, high = bounds[q]
            count = high - low
            padded = round_up(count, 16)
            group = group_of(count)

            for offset in [None] + peers:
                if offset is None:
                    origin, block = me, send_in
                else:
                    origin, block = peer(offset), recv_in
                    arrival(0, q, offset).wait_recv()
                if padded != count:
                    unpack[pl.ds(count * rows, (padded - count) * rows)] = jnp.zeros(
                        ((padded - count) * rows, width), jnp.float32
                    )

                def widen(t, carry):
                    value = block[origin, pl.ds(low + t * group, group)]
                    unpack[pl.ds(pl.multiple_of(t * group * rows, 8), group * rows)] = value.astype(
                        jnp.float32
                    ).reshape(group * rows, width)
                    return carry

                lax.fori_loop(0, count // group, widen, 0)
                base = pl.multiple_of(origin * own_pad + low, 16)
                for i in range(rows):
                    flat[pl.ds(base, padded), pl.ds(i * width, width)] = unpack[
                        pl.ds(i, padded, stride=rows)
                    ].astype(jnp.bfloat16)

        start = 0
        for q in range(chunks):
            low, high = bounds[q]
            count = high - low
            tall = round_up(count, 16)
            group = group_of(count)
            total = parts * tall

            def multiply(pair, carry):
                columns = pl.ds(pl.multiple_of(pair * 2 * width, 2 * width), 2 * width)
                result = jnp.dot(
                    weight_buf[start : start + total],
                    flat[:, columns],
                    preferred_element_type=jnp.float32,
                )
                spread[pl.ds(pair * 2, total, stride=rows)] = result[:, :width]
                spread[pl.ds(pair * 2 + 1, total, stride=rows)] = result[:, width:]
                return carry

            lax.fori_loop(0, rows // 2, multiply, 0)
            if not step == steps - 1:
                for offset in peers:
                    exchange(1, q, offset).wait_send()
            for offset in peers + [None]:
                part = me if offset is None else peer(offset)
                target = recv_out if offset is None else send_out

                def narrow(t, carry):
                    place = pl.multiple_of((part * tall + t * group) * rows, 8)
                    value = spread[pl.ds(place, group * rows)]
                    target[part, pl.ds(low + t * group, group)] = value.reshape(
                        group, rows, width
                    ).astype(jnp.bfloat16)
                    return carry

                lax.fori_loop(0, count // group, narrow, 0)
                if offset is not None:
                    exchange(1, q, offset).start()
            start += total

        forcing = None if last else forcing_of(step - 1)
        for q in range(chunks):
            low, high = bounds[q]
            count = high - low
            position = (steps - 1 - step) * chunks + q
            slot = position % 2
            source_copy(position).wait()
            for offset in peers:
                arrival(1, q, offset).wait_recv()

            def update(c, carry):
                to_west, to_east = carry
                coupled = jnp.concatenate(
                    [recv_out[part, c].astype(jnp.float32) for part in range(parts)], axis=0
                )
                factor = source_buf[slot, c - low].astype(jnp.float32)
                adjoint = state[c] + factor * coupled
                state[c] = adjoint
                to_west = jnp.where(lane == 0, adjoint, pltpu.roll(to_west, 1, 1))
                to_east = jnp.where(lane == width - 1, adjoint, pltpu.roll(to_east, width - 1, 1))
                return to_west, to_east

            zero = jnp.zeros((lat, width), jnp.float32)
            to_west, to_east = lax.fori_loop(low, high, update, (zero, zero))
            halo_send[position, 0] = to_west
            halo_send[position, 1] = to_east
            halo(position, 0).start()
            halo(position, 1).start()
            if position + 2 < len(order):
                source_copy(position + 2).start()
            if not last:
                for offset in peers:
                    exchange(0, q, offset).wait_send()
            halo(position, 0).wait()
            halo(position, 1).wait()

            def advect(c, carry):
                from_east, from_west = carry
                adjoint = state[c]
                speed_x = drift_x[me * own + c]
                speed_y = drift_y[me * own + c]
                eastern = jnp.where(lane == width - 1, from_east, pltpu.roll(adjoint, width - 1, 1))
                western = jnp.where(lane == 0, from_west, pltpu.roll(adjoint, 1, 1))
                northern = jnp.where(row == lat - 1, 0.0, pltpu.roll(adjoint, lat - 1, 0))
                southern = jnp.where(row == 0, 0.0, pltpu.roll(adjoint, 1, 0))
                stay = 1.0 - jnp.abs(speed_x) - jnp.abs(speed_y)
                result = (
                    stay * adjoint
                    + jnp.maximum(speed_x, 0.0) * eastern
                    + jnp.maximum(-speed_x, 0.0) * western
                )
                result = (
                    result
                    + jnp.maximum(speed_y, 0.0) * northern
                    + jnp.maximum(-speed_y, 0.0) * southern
                )
                if last:
                    state[c] = result
                else:
                    emit((result + forcing) * ocean, c)
                return pltpu.roll(from_east, 1, 1), pltpu.roll(from_west, width - 1, 1)

            from_east = pltpu.roll(halo_recv[position, 0], (width - count) % width, 1)
            from_west = pltpu.roll(halo_recv[position, 1], count % width, 1)
            lax.fori_loop(low, high, advect, (from_east, from_west))
            if last:
                out_copy(q).start()
            else:
                for offset in peers:
                    exchange(0, q, offset).start()

    for q in range(chunks):
        for offset in peers:
            exchange(0, q, offset).wait_send()
            exchange(1, q, offset).wait_send()
        out_copy(q).wait()


def per_device(
    parts, ring, lam_final, stored_source, mixing, drift_x, drift_y, ocean_mask, misfit, obs_mask
):
    steps = stored_source.shape[0]
    own, lat, width = lam_final.shape
    rows = lat // parts
    bounds = chunk_bounds(own)
    own_pad = round_up(own, 128)
    largest = max(high - low for low, high in bounds)
    tall = sum(round_up(high - low, 16) for low, high in bounds) * parts
    vmem = pl.BlockSpec(memory_space=pltpu.VMEM)
    smem = pl.BlockSpec(memory_space=pltpu.SMEM)
    hbm = pl.BlockSpec(memory_space=pl.ANY)
    block = pltpu.VMEM((parts, own, rows, width), jnp.bfloat16)
    dma = pltpu.SemaphoreType.DMA
    positions = steps * CHUNKS
    return pl.pallas_call(
        functools.partial(kernel, steps, parts, ring, bounds, own_pad),
        out_shape=jax.ShapeDtypeStruct(lam_final.shape, jnp.float32),
        in_specs=[hbm, hbm, hbm, smem, smem, vmem, vmem, vmem],
        out_specs=hbm,
        scratch_shapes=[
            pltpu.VMEM((own, lat, width), jnp.float32),
            block, block, block, block,
            pltpu.VMEM((parts * own_pad, rows * width), jnp.bfloat16),
            pltpu.VMEM(mixing.shape, jnp.bfloat16),
            pltpu.VMEM((tall, parts * own), jnp.bfloat16),
            pltpu.VMEM((tall, parts * own_pad), jnp.bfloat16),
            pltpu.VMEM((parts * round_up(largest, 16) * rows, width), jnp.float32),
            pltpu.VMEM((round_up(largest, 16) * rows, width), jnp.float32),
            pltpu.VMEM((2, largest, lat, width), jnp.bfloat16),
            pltpu.VMEM((positions, 2, lat, width), jnp.float32),
            pltpu.VMEM((positions, 2, lat, width), jnp.float32),
            dma((2, CHUNKS, parts - 1)),
            dma((2, CHUNKS, parts)),
            dma((positions, 2)),
            dma((positions, 2)),
            dma((CHUNKS,)),
            dma((2,)),
            dma,
            dma((CHUNKS,)),
        ],
        compiler_params=pltpu.CompilerParams(
            collective_id=0, has_side_effects=True, vmem_limit_bytes=60 * 1024 * 1024
        ),
    )(lam_final, stored_source, mixing, drift_x, drift_y, ocean_mask, misfit, obs_mask)


def solution(mesh):
    in_specs = (
        P("spec", None, "lon"),
        P(None, "spec", None, "lon"),
        P(),
        P(),
        P(),
        P(None, "lon"),
        P(None, None, "lon"),
        P(None, None, "lon"),
    )
    out_specs = P("spec", None, "lon")
    return jax.shard_map(
        functools.partial(per_device, mesh.shape["spec"], mesh.shape["lon"]),
        mesh=mesh, in_specs=in_specs, out_specs=out_specs, check_vma=False,
    )
```
